32 devices in a mesh: tbl: 8 (over z, core), grp: 4 (over y, x).
Axes of the slice: x: 2, y: 2, z: 4, core: 2. Of those that a mesh axis runs over, the one named last changes fastest.
Arguments:
- codes: bfloat16 [8, 1024, 256], P('tbl', 'grp'), may hold values from -4 to 4
- row_scales: float32 [8, 1024], P('tbl', 'grp'), may hold values from 0.25 to 16
- history_lengths: int32 [32, 8], P(None, 'tbl'), may hold values from 1 to 32, as said below
- history_ids: int32 [32, 8, 32], P(None, 'tbl'), may hold values from 0 to 1023, as said below
- query_items: int32 [32, 8], P(None, 'tbl'), may hold values from 0 to 1023, as said below
- slot_tables: int32 [8], replicated, may hold values from 0 to 7, each once
Outputs:
- pooled: bfloat16 [32, 8, 256], P(('tbl', 'grp'))
The draws below stay inside these ranges and needn't reach their ends.
Inputs may be any that keep to these rules, and one draw needn't show every extreme that they name: `history_lengths`: the largest length, 32, occurs in every draw. `history_ids`: entries at positions at or beyond the history's length are row ids too, and are to be ignored. query_items[b, s] equals history_ids[b, s, h] for some h below history_lengths[b, s].
All inputs are finite; a program needn't handle non-finite values.
Results may differ from the reference program's by a relative error of at most 0.004.
Values may be sent and summed in bfloat16 or wider, within the bound.
A program may use at most 64 MiB of HBM per device.

```python
import math
import jax
import jax.numpy as jnp
from jax import lax

E = 256
ROWS_DEV = 256
HMAX = 32
NT = 8
TROWS = 1024
BATCH = 32


def history_draw(key):
    length_key, owner_key, row_key, where_key = jax.random.split(jax.random.fold_in(key, 7), 4)
    lengths = jax.random.randint(length_key, (BATCH, NT), 1, HMAX + 1)
    sample_pos = jnp.arange(BATCH, dtype=jnp.int32)[:, None]
    slot_pos = jnp.arange(NT, dtype=jnp.int32)[None, :]
    lengths = jnp.where((sample_pos + 3 * slot_pos) % 61 == 0, HMAX, lengths)
    groups = TROWS // ROWS_DEV
    picked = jax.random.randint(owner_key, (BATCH, NT, HMAX), 0, 2 * groups)
    owner = (jnp.minimum(picked, groups - 1) + slot_pos[:, :, None]) % groups
    ids = owner * ROWS_DEV + jax.random.randint(row_key, (BATCH, NT, HMAX), 0, ROWS_DEV)
    target_pos = jax.random.randint(where_key, (BATCH, NT), 0, 1 << 20) % lengths
    target = jnp.take_along_axis(ids, target_pos[:, :, None], axis=2)[:, :, 0]
    partner_pos = (target_pos + 1) % lengths
    positions = jnp.arange(HMAX, dtype=jnp.int32)[None, None, :]
    pairing = (positions == partner_pos[:, :, None]) & (lengths[:, :, None] > 1)
    ids = jnp.where(pairing, jnp.bitwise_xor(target, 1)[:, :, None], ids)
    return (lengths.astype(jnp.int32), ids.astype(jnp.int32), target.astype(jnp.int32))


def draw_history_lengths(key, part):
    return history_draw(key)[0]


def draw_history_ids(key, part):
    return history_draw(key)[1]


def draw_query_items(key, part):
    return history_draw(key)[2]


def draw_codes(key, part):
    base_key = jax.random.fold_in(jax.random.fold_in(key, 11), 0)
    base = jnp.clip(jax.random.normal(base_key, (NT, TROWS, E), jnp.float32), -4.0, 4.0)
    return base.astype(jnp.bfloat16)


def draw_row_scales(key, part):
    first_key = jax.random.fold_in(jax.random.fold_in(key, 13), 0)
    return jnp.exp(jax.random.uniform(first_key, (NT, TROWS), jnp.float32, math.log(0.25), math.log(2.0)))


def setup_inputs(seed: int = 0) -> dict:
    splits = jax.random.split(jax.random.key(seed), 7)
    return {
        "codes": draw_codes(jax.random.fold_in(splits[6], 71), 0),
        "row_scales": draw_row_scales(jax.random.fold_in(splits[6], 71), 0),
        "history_lengths": draw_history_lengths(jax.random.fold_in(splits[6], 71), 0),
        "history_ids": draw_history_ids(jax.random.fold_in(splits[6], 71), 0),
        "query_items": draw_query_items(jax.random.fold_in(splits[6], 71), 0),
        "slot_tables": jax.random.permutation(splits[5], NT).astype(jnp.int32),
    }


def reference(codes, row_scales, history_lengths, history_ids, query_items, slot_tables):
    positions = jnp.arange(HMAX, dtype=jnp.int32)

    def one_slot(inputs):
        table, factors, ids, lengths, items = inputs
        found = jnp.take(table, ids, axis=0).astype(jnp.float32)
        factor = jnp.take(factors, ids, axis=0)
        query = jnp.take(table, items, axis=0).astype(jnp.float32) * jnp.take(factors, items, axis=0)[:, None]
        raw = jnp.einsum("bhe,be->bh", found, query, precision=lax.Precision.HIGHEST)
        score = raw * factor / E
        keep = positions[None, :] < lengths[:, None]
        peak = jnp.max(jnp.where(keep, score, -1e30), axis=1)
        weight = jnp.where(keep, jnp.exp(score - peak[:, None]), 0.0)
        weighted = jnp.einsum("bh,bhe->be", weight * factor, found, precision=lax.Precision.HIGHEST)
        return weighted / jnp.sum(weight, axis=1)[:, None]

    pooled_slot = lax.map(one_slot, (codes, row_scales, jnp.transpose(history_ids, (1, 0, 2)),
                                     jnp.transpose(history_lengths), jnp.transpose(query_items)))
    arranged = jnp.transpose(pooled_slot, (1, 0, 2)).astype(jnp.bfloat16)
    inverse = jnp.argsort(slot_tables).astype(jnp.int32)
    return jnp.take(arranged, inverse, axis=1)
```

```python
import functools

import jax
import jax.numpy as jnp
from jax import lax
from jax.experimental import pallas as pl
from jax.experimental.pallas import tpu as pltpu
from jax.sharding import PartitionSpec as P

LANES = 128
UNROLL = 64


def each(count, body):
    if count <= UNROLL:
        for k in range(1, count):
            body(k)
    else:
        lax.fori_loop(1, count, lambda k, c: (body(k), c)[1], 0)


def column(row):
    n = row.shape[1]
    same = lax.broadcasted_iota(jnp.int32, (n, n), 0) == lax.broadcasted_iota(jnp.int32, (n, n), 1)
    return jnp.sum(jnp.where(same, row, 0), axis=1, keepdims=True)


def kernel(
    tbl_n, grp_n, block,
    codes_hbm, scales_hbm, lengths_hbm, ids_hbm, items_hbm, tables_hbm,
    out_ref,
    codes, scales, lengths, ids, items, tables, query, query_in, counts, outbox, inbox,
    load_sem, table_sem, query_send, query_recv, send_sem, recv_sem,
):
    rows, emb = codes.shape
    batch, _, history = ids.shape
    owned = batch // (tbl_n * grp_n)
    n_dev = tbl_n * grp_n
    tbl_i = lax.axis_index("tbl")
    grp_i = lax.axis_index("grp")
    me = tbl_i * grp_n + grp_i

    loads = [
        pltpu.make_async_copy(src, dst, load_sem.at[i])
        for i, (src, dst) in enumerate(
            ((items_hbm, items), (codes_hbm, codes), (scales_hbm, scales),
             (lengths_hbm, lengths), (ids_hbm, ids))
        )
    ]
    for load in loads:
        load.start()
    table_load = pltpu.make_async_copy(tables_hbm, tables, table_sem)
    table_load.start()

    barrier = pltpu.get_barrier_semaphore()

    def greet(k):
        pl.semaphore_signal(
            barrier, inc=1, device_id=lax.rem(me + k, n_dev),
            device_id_type=pl.DeviceIdType.LOGICAL,
        )

    each(n_dev, greet)
    for load in loads:
        load.wait()

    row_scale = scales[...]
    offset = grp_i * rows
    lane_rows = lax.broadcasted_iota(jnp.int32, (block, rows), 1)
    lane = lax.broadcasted_iota(jnp.int32, (block, LANES), 1)
    blocks = [pl.ds(b * block, block) for b in range(batch // block)]

    for at in blocks:
        hit = column(items[:, at]) - offset == lane_rows
        found = jnp.dot(
            jnp.where(hit, 1.0, 0.0).astype(jnp.bfloat16), codes[...],
            preferred_element_type=jnp.float32,
        )
        factor = jnp.sum(jnp.where(hit, row_scale, 0.0), axis=1, keepdims=True)
        high = factor.astype(jnp.bfloat16).astype(jnp.float32)
        middle = (factor - high).astype(jnp.bfloat16).astype(jnp.float32)
        low = factor - high - middle
        query[at, :emb] = found.astype(jnp.bfloat16)
        query[at, emb:] = jnp.where(
            lane == 0, high, jnp.where(lane == 1, middle, jnp.where(lane == 2, low, 0.0))
        ).astype(jnp.bfloat16)

    pl.semaphore_wait(barrier, n_dev - 1)

    def ask(k):
        pltpu.make_async_remote_copy(
            src_ref=query, dst_ref=query_in.at[k - 1],
            send_sem=query_send, recv_sem=query_recv,
            device_id=tbl_i * grp_n + lax.rem(grp_i + k, grp_n),
            device_id_type=pl.DeviceIdType.LOGICAL,
        ).start()

    each(grp_n, ask)

    for at in blocks:
        local = ids[at, 0, :] - offset
        positions = lax.broadcasted_iota(jnp.int32, (block, history), 1)
        local = jnp.where(positions < column(lengths[:, at]), local, -1)
        total = jnp.zeros((block, rows), jnp.float32)
        for h in range(history):
            total += jnp.where(local[:, h:h + 1] == lane_rows, 1.0, 0.0)
        counts[at, :] = total

    arrived = pltpu.make_async_copy(query_in, query_in, query_recv)
    arrived.wait()

    for b, at in enumerate(blocks):
        asked = query[at, :]
        for k in range(grp_n - 1):
            asked += query_in[k, at, :]
        parts = asked[:, emb:].astype(jnp.float32)
        factor = parts[:, 0:1] + parts[:, 1:2] + parts[:, 2:3]
        raw = lax.dot_general(
            asked[:, :emb], codes[...], (((1,), (1,)), ((), ())),
            preferred_element_type=jnp.float32,
        )
        number = counts[at, :]
        score = jnp.where(number > 0.0, raw * factor * row_scale / emb, -1e30)
        peak = jnp.max(score, axis=1, keepdims=True)
        weight = number * jnp.exp(score - peak)
        mass = jnp.sum(weight, axis=1, keepdims=True)
        weight = weight * row_scale
        high = weight.astype(jnp.bfloat16)
        low = (weight - high.astype(jnp.float32)).astype(jnp.bfloat16)
        both = jnp.dot(
            jnp.concatenate([high, low], axis=0), codes[...],
            preferred_element_type=jnp.float32,
        )
        sums = both[:block] + both[block:]
        ends = jnp.where(lane == 0, peak, mass)
        for r in range(block):
            device, place = divmod(b * block + r, owned)
            outbox[device, place:place + 1, :emb] = sums[r:r + 1, :]
            outbox[device, place:place + 1, emb:] = ends[r:r + 1, :]

    slot = grp_i * tbl_n + tbl_i

    def give(k):
        target = lax.rem(me + k, n_dev)
        pltpu.make_async_remote_copy(
            src_ref=outbox.at[target], dst_ref=inbox.at[slot],
            send_sem=send_sem, recv_sem=recv_sem,
            device_id=target, device_id_type=pl.DeviceIdType.LOGICAL,
        ).start()

    each(n_dev, give)
    own = pltpu.make_async_copy(outbox.at[me], inbox.at[slot], recv_sem)
    own.start()
    table_load.wait()
    pltpu.make_async_copy(query_in, query_in, query_send).wait()
    pltpu.make_async_copy(inbox, inbox, recv_sem).wait()

    out_rows = lax.broadcasted_iota(jnp.int32, (tbl_n, emb), 0)
    for o in range(owned):
        shares = [inbox[pl.ds(g * tbl_n, tbl_n), o, :] for g in range(grp_n)]
        peak = shares[0][:, emb:emb + 1]
        for share in shares[1:]:
            peak = jnp.maximum(peak, share[:, emb:emb + 1])
        mass = jnp.zeros((tbl_n, 1), jnp.float32)
        sums = jnp.zeros((tbl_n, emb), jnp.float32)
        for share in shares:
            scale = jnp.exp(share[:, emb:emb + 1] - peak)
            mass += share[:, emb + 1:emb + 2] * scale
            sums += share[:, :emb] * scale
        pooled = sums / mass
        result = jnp.zeros((tbl_n, emb), jnp.float32)
        for s in range(tbl_n):
            result = jnp.where(out_rows == tables[s], pooled[s:s + 1, :], result)
        out_ref[o] = result.astype(jnp.bfloat16)
    sent = outbox.at[pl.ds(0, n_dev - 1)]
    pltpu.make_async_copy(sent, sent, send_sem).wait()


def per_device(tbl_n, grp_n, codes, row_scales, history_lengths, history_ids, query_items, slot_tables):
    _, rows, emb = codes.shape
    batch, _, history = history_ids.shape
    n_dev = tbl_n * grp_n
    owned = batch // n_dev
    block = min(32, batch)
    wide = emb + LANES
    hbm = pl.BlockSpec(memory_space=pl.ANY)
    return pl.pallas_call(
        functools.partial(kernel, tbl_n, grp_n, block),
        out_shape=jax.ShapeDtypeStruct((owned, tbl_n, emb), jnp.bfloat16),
        in_specs=[hbm] * 6,
        out_specs=pl.BlockSpec(memory_space=pltpu.VMEM),
        scratch_shapes=[
            pltpu.VMEM((rows, emb), codes.dtype),
            pltpu.VMEM((1, rows), jnp.float32),
            pltpu.VMEM((1, batch), jnp.int32),
            pltpu.VMEM((batch, 1, history), jnp.int32),
            pltpu.VMEM((1, batch), jnp.int32),
            pltpu.SMEM((tbl_n,), jnp.int32),
            pltpu.VMEM((batch, wide), jnp.bfloat16),
            pltpu.VMEM((grp_n - 1, batch, wide), jnp.bfloat16),
            pltpu.VMEM((batch, rows), jnp.float32),
            pltpu.VMEM((n_dev, owned, wide), jnp.float32),
            pltpu.VMEM((n_dev, owned, wide), jnp.float32),
            pltpu.SemaphoreType.DMA((5,)),
            pltpu.SemaphoreType.DMA,
            pltpu.SemaphoreType.DMA,
            pltpu.SemaphoreType.DMA,
            pltpu.SemaphoreType.DMA,
            pltpu.SemaphoreType.DMA,
        ],
        compiler_params=pltpu.CompilerParams(collective_id=0, has_side_effects=True),
    )(
        codes.reshape(rows, emb), row_scales, history_lengths.T, history_ids,
        query_items.T, slot_tables,
    )


def solution(mesh):
    placed = (
        P("tbl", "grp", None),
        P("tbl", "grp"),
        P(None, "tbl"),
        P(None, "tbl", None),
        P(None, "tbl"),
        P(),
    )
    return jax.shard_map(
        functools.partial(per_device, mesh.shape["tbl"], mesh.shape["grp"]),
        mesh=mesh,
        in_specs=placed,
        out_specs=P(("tbl", "grp"), None, None),
        check_vma=False,
    )
```

```python
import functools

import jax
import jax.numpy as jnp
from jax import lax
from jax.experimental import pallas as pl
from jax.experimental.pallas import tpu as pltpu
from jax.sharding import PartitionSpec as P

LANES = 128
LOGICAL = pl.DeviceIdType.LOGICAL
UNROLL = 64


def each(count, body):
    if count <= UNROLL:
        for k in range(1, count):
            body(k)
    else:
        lax.fori_loop(1, count, lambda k, c: (body(k), c)[1], 0)


def column(row):
    n = row.shape[1]
    same = lax.broadcasted_iota(jnp.int32, (n, n), 0) == lax.broadcasted_iota(jnp.int32, (n, n), 1)
    return jnp.sum(jnp.where(same, row, 0), axis=1, keepdims=True)


def kernel(
    tbl_n, grp_n, block,
    codes_hbm, scales_hbm, lengths_hbm, ids_hbm, items_hbm, tables_hbm,
    out_ref,
    codes, scales, lengths, ids, items, tables, query, query_in, scales_in, factors, counts,
    outbox, inbox,
    load_sem, table_sem, query_send, query_recv, scales_send, scales_recv, send_sem, recv_sem,
    ready,
):
    rows, emb = codes.shape
    batch, _, history = ids.shape
    owned = batch // (tbl_n * grp_n)
    n_dev = tbl_n * grp_n
    tbl_i = lax.axis_index("tbl")
    grp_i = lax.axis_index("grp")
    me = tbl_i * grp_n + grp_i

    pairs = (
        (items_hbm, items), (codes_hbm, codes), (scales_hbm, scales),
        (lengths_hbm, lengths), (ids_hbm, ids),
    )
    loads = [
        pltpu.make_async_copy(src, dst, load_sem.at[i]) for i, (src, dst) in enumerate(pairs)
    ]
    for load in loads:
        load.start()
    items_load, codes_load, scales_load, lengths_load, ids_load = loads
    table_load = pltpu.make_async_copy(tables_hbm, tables, table_sem)
    table_load.start()

    barrier = pltpu.get_barrier_semaphore()

    tbl_bits = [1 << i for i in range(tbl_n.bit_length() - 1)]
    grp_peers = [tbl_i * grp_n + lax.rem(grp_i + k, grp_n) for k in range(1, grp_n)]
    tbl_peers = [lax.bitwise_xor(tbl_i, bit) * grp_n + grp_i for bit in tbl_bits]
    for peer in grp_peers + tbl_peers:
        pl.semaphore_signal(barrier, inc=1, device_id=peer, device_id_type=LOGICAL)

    lane_rows = lax.broadcasted_iota(jnp.int32, (block, rows), 1)
    blocks = [pl.ds(b * block, block) for b in range(batch // block)]
    offset = grp_i * rows

    items_load.wait()
    codes_load.wait()
    for at in blocks:
        hit = column(items[:, at]) - offset == lane_rows
        found = jnp.dot(
            jnp.where(hit, 1.0, 0.0).astype(jnp.bfloat16), codes[...],
            preferred_element_type=jnp.float32,
        )
        query[at, :] = found.astype(jnp.bfloat16)
    scales_load.wait()

    pl.semaphore_wait(barrier, len(grp_peers) + len(tbl_peers))

    for k, peer in enumerate(grp_peers):
        pltpu.make_async_remote_copy(
            src_ref=query, dst_ref=query_in.at[k],
            send_sem=query_send, recv_sem=query_recv,
            device_id=peer, device_id_type=LOGICAL,
        ).start()
    for k, peer in enumerate(grp_peers):
        pltpu.make_async_remote_copy(
            src_ref=scales, dst_ref=scales_in.at[k],
            send_sem=scales_send, recv_sem=scales_recv,
            device_id=peer, device_id_type=LOGICAL,
        ).start()

    def tell(i):
        pl.semaphore_signal(
            ready.at[i], inc=1, device_id=tbl_peers[i], device_id_type=LOGICAL
        )

    tell(0)
    lengths_load.wait()
    ids_load.wait()
    row_scale = scales[...]
    lane = lax.broadcasted_iota(jnp.int32, (block, LANES), 1)
    for at in blocks:
        local = ids[at, 0, :] - offset
        positions = lax.broadcasted_iota(jnp.int32, (block, history), 1)
        local = jnp.where(positions < column(lengths[:, at]), local, -1)
        total = jnp.zeros((block, rows), jnp.float32)
        for h in range(history):
            total += jnp.where(local[:, h:h + 1] == lane_rows, 1.0, 0.0)
        counts[at, :] = total

    for i in range(len(tbl_bits)):
        pl.semaphore_wait(ready.at[i], 1)
        if i + 1 < len(tbl_bits):
            tell(i + 1)

    pltpu.make_async_copy(scales_in, scales_in, scales_recv).wait()
    for at in blocks:
        wanted = column(items[:, at])
        total = jnp.where(wanted - offset == lane_rows, row_scale, 0.0)
        for k in range(grp_n - 1):
            theirs = lax.rem(grp_i + grp_n - 1 - k, grp_n) * rows
            total += jnp.where(wanted - theirs == lane_rows, scales_in[k], 0.0)
        factors[at, :] = jnp.sum(total, axis=1, keepdims=True)

    pltpu.make_async_copy(query_in, query_in, query_recv).wait()

    for b, at in enumerate(blocks):
        asked = query[at, :]
        for k in range(grp_n - 1):
            asked += query_in[k, at, :]
        factor = factors[at, :]
        raw = lax.dot_general(
            asked, codes[...], (((1,), (1,)), ((), ())),
            preferred_element_type=jnp.float32,
        )
        number = counts[at, :]
        score = jnp.where(number > 0.0, raw * factor * row_scale / emb, -1e30)
        peak = jnp.max(score, axis=1, keepdims=True)
        weight = number * jnp.exp(score - peak)
        mass = jnp.sum(weight, axis=1, keepdims=True)
        weight = weight * row_scale
        high = weight.astype(jnp.bfloat16)
        low = (weight - high.astype(jnp.float32)).astype(jnp.bfloat16)
        both = jnp.dot(
            jnp.concatenate([high, low], axis=0), codes[...],
            preferred_element_type=jnp.float32,
        )
        sums = both[:block] + both[block:]
        ends = jnp.where(lane == 0, peak, mass)
        for r in range(block):
            device, place = divmod(b * block + r, owned)
            outbox[device, place:place + 1, :emb] = sums[r:r + 1, :]
            outbox[device, place:place + 1, emb:] = ends[r:r + 1, :]

    slot = grp_i * tbl_n + tbl_i

    def give(k):
        target = lax.rem(me + k, n_dev)
        pltpu.make_async_remote_copy(
            src_ref=outbox.at[target], dst_ref=inbox.at[slot],
            send_sem=send_sem, recv_sem=recv_sem,
            device_id=target, device_id_type=LOGICAL,
        ).start()

    each(n_dev, give)
    own = pltpu.make_async_copy(outbox.at[me], inbox.at[slot], recv_sem)
    own.start()
    table_load.wait()
    pltpu.make_async_copy(query_in, query_in, query_send).wait()
    pltpu.make_async_copy(scales_in, scales_in, scales_send).wait()
    pltpu.make_async_copy(inbox, inbox, recv_sem).wait()

    out_rows = lax.broadcasted_iota(jnp.int32, (tbl_n, emb), 0)
    for o in range(owned):
        shares = [inbox[pl.ds(g * tbl_n, tbl_n), o, :] for g in range(grp_n)]
        peak = shares[0][:, emb:emb + 1]
        for share in shares[1:]:
            peak = jnp.maximum(peak, share[:, emb:emb + 1])
        mass = jnp.zeros((tbl_n, 1), jnp.float32)
        sums = jnp.zeros((tbl_n, emb), jnp.float32)
        for share in shares:
            scale = jnp.exp(share[:, emb:emb + 1] - peak)
            mass += share[:, emb + 1:emb + 2] * scale
            sums += share[:, :emb] * scale
        pooled = sums / mass
        result = jnp.zeros((tbl_n, emb), jnp.float32)
        for s in range(tbl_n):
            result = jnp.where(out_rows == tables[s], pooled[s:s + 1, :], result)
        out_ref[o] = result.astype(jnp.bfloat16)
    sent = outbox.at[pl.ds(0, n_dev - 1)]
    pltpu.make_async_copy(sent, sent, send_sem).wait()


def store(pooled, out_hbm, sem):
    out = pltpu.make_async_copy(pooled, out_hbm, sem)
    out.start()
    out.wait()


def per_device(tbl_n, grp_n, codes, row_scales, history_lengths, history_ids, query_items, slot_tables):
    _, rows, emb = codes.shape
    batch, _, history = history_ids.shape
    n_dev = tbl_n * grp_n
    owned = batch // n_dev
    block = min(32, batch)
    wide = emb + LANES
    hbm = pl.BlockSpec(memory_space=pl.ANY)
    pooled = pl.pallas_call(
        functools.partial(kernel, tbl_n, grp_n, block),
        out_shape=pltpu.VMEM((owned, tbl_n, emb), jnp.bfloat16),
        in_specs=[hbm] * 6,
        out_specs=pl.BlockSpec(memory_space=pltpu.VMEM),
        scratch_shapes=[
            pltpu.VMEM((rows, emb), codes.dtype),
            pltpu.VMEM((1, rows), jnp.float32),
            pltpu.VMEM((1, batch), jnp.int32),
            pltpu.VMEM((batch, 1, history), jnp.int32),
            pltpu.VMEM((1, batch), jnp.int32),
            pltpu.SMEM((tbl_n,), jnp.int32),
            pltpu.VMEM((batch, emb), jnp.bfloat16),
            pltpu.VMEM((grp_n - 1, batch, emb), jnp.bfloat16),
            pltpu.VMEM((grp_n - 1, 1, rows), jnp.float32),
            pltpu.VMEM((batch, 1), jnp.float32),
            pltpu.VMEM((batch, rows), jnp.float32),
            pltpu.VMEM((n_dev, owned, wide), jnp.float32),
            pltpu.VMEM((n_dev, owned, wide), jnp.float32),
            pltpu.SemaphoreType.DMA((5,)),
            pltpu.SemaphoreType.DMA,
            pltpu.SemaphoreType.DMA,
            pltpu.SemaphoreType.DMA,
            pltpu.SemaphoreType.DMA,
            pltpu.SemaphoreType.DMA,
            pltpu.SemaphoreType.DMA,
            pltpu.SemaphoreType.DMA,
            pltpu.SemaphoreType.REGULAR((tbl_n.bit_length() - 1,)),
        ],
        compiler_params=pltpu.CompilerParams(collective_id=0, has_side_effects=True),
    )(
        codes.reshape(rows, emb), row_scales, history_lengths.T, history_ids,
        query_items.T, slot_tables,
    )
    return pl.pallas_call(
        store,
        out_shape=jax.ShapeDtypeStruct((owned, tbl_n, emb), jnp.bfloat16),
        in_specs=[pl.BlockSpec(memory_space=pltpu.VMEM)],
        out_specs=pl.BlockSpec(memory_space=pl.ANY),
        scratch_shapes=[pltpu.SemaphoreType.DMA],
    )(pltpu.with_memory_space_constraint(pooled, pltpu.VMEM))


def solution(mesh):
    placed = (
        P("tbl", "grp", None),
        P("tbl", "grp"),
        P(None, "tbl"),
        P(None, "tbl", None),
        P(None, "tbl"),
        P(),
    )
    return jax.shard_map(
        functools.partial(per_device, mesh.shape["tbl"], mesh.shape["grp"]),
        mesh=mesh,
        in_specs=placed,
        out_specs=P(("tbl", "grp"), None, None),
        check_vma=False,
    )
```

```python
import functools

import jax
import jax.numpy as jnp
from jax import lax
from jax.experimental import pallas as pl
from jax.experimental.pallas import tpu as pltpu
from jax.sharding import PartitionSpec as P

LANES = 128
LOGICAL = pl.DeviceIdType.LOGICAL
UNROLL = 64


def each(count, body):
    if count <= UNROLL:
        for k in range(1, count):
            body(k)
    else:
        lax.fori_loop(1, count, lambda k, c: (body(k), c)[1], 0)


def column(row):
    n = row.shape[1]
    same = lax.broadcasted_iota(jnp.int32, (n, n), 0) == lax.broadcasted_iota(jnp.int32, (n, n), 1)
    return jnp.sum(jnp.where(same, row, 0), axis=1, keepdims=True)


def kernel(
    tbl_n, grp_n, block,
    codes_hbm, scales_hbm, lengths_hbm, ids_hbm, items_hbm, tables_hbm,
    out_ref,
    codes, scales, lengths, ids, items, tables, query, query_in, scales_in, factors, counts,
    outbox, inbox,
    load_sem, table_sem, query_send, query_recv, scales_send, scales_recv, send_sem, recv_sem,
    ready,
):
    rows, emb = codes.shape
    batch, _, history = ids.shape
    owned = batch // (tbl_n * grp_n)
    n_dev = tbl_n * grp_n
    tbl_i = lax.axis_index("tbl")
    grp_i = lax.axis_index("grp")
    me = tbl_i * grp_n + grp_i

    pairs = (
        (items_hbm, items), (codes_hbm, codes), (scales_hbm, scales),
        (lengths_hbm, lengths), (ids_hbm, ids),
    )
    loads = [
        pltpu.make_async_copy(src, dst, load_sem.at[i]) for i, (src, dst) in enumerate(pairs)
    ]
    for load in loads:
        load.start()
    items_load, codes_load, scales_load, lengths_load, ids_load = loads
    table_load = pltpu.make_async_copy(tables_hbm, tables, table_sem)
    table_load.start()

    barrier = pltpu.get_barrier_semaphore()

    tbl_bits = [1 << i for i in range(tbl_n.bit_length() - 1)]
    grp_peers = [tbl_i * grp_n + lax.rem(grp_i + k, grp_n) for k in range(1, grp_n)]
    tbl_peers = [lax.bitwise_xor(tbl_i, bit) * grp_n + grp_i for bit in tbl_bits]
    for peer in grp_peers + tbl_peers:
        pl.semaphore_signal(barrier, inc=1, device_id=peer, device_id_type=LOGICAL)

    lane_rows = lax.broadcasted_iota(jnp.int32, (block, rows), 1)
    blocks = [pl.ds(b * block, block) for b in range(batch // block)]
    offset = grp_i * rows

    items_load.wait()
    codes_load.wait()
    for at in blocks:
        hit = column(items[:, at]) - offset == lane_rows
        found = jnp.dot(
            jnp.where(hit, 1.0, 0.0).astype(jnp.bfloat16), codes[...],
            preferred_element_type=jnp.float32,
        )
        query[at, :] = found.astype(jnp.bfloat16)
    scales_load.wait()

    pl.semaphore_wait(barrier, len(grp_peers) + len(tbl_peers))

    for half in range(2):
        part = pl.ds(half * (batch // 2), batch // 2)
        for k, peer in enumerate(grp_peers):
            pltpu.make_async_remote_copy(
                src_ref=query.at[part], dst_ref=query_in.at[half, k],
                send_sem=query_send, recv_sem=query_recv.at[half],
                device_id=peer, device_id_type=LOGICAL,
            ).start()
    for k, peer in enumerate(grp_peers):
        pltpu.make_async_remote_copy(
            src_ref=scales, dst_ref=scales_in.at[k],
            send_sem=scales_send, recv_sem=scales_recv,
            device_id=peer, device_id_type=LOGICAL,
        ).start()

    def tell(i):
        pl.semaphore_signal(
            ready.at[i], inc=1, device_id=tbl_peers[i], device_id_type=LOGICAL
        )

    tell(0)
    lengths_load.wait()
    ids_load.wait()
    row_scale = scales[...]
    lane = lax.broadcasted_iota(jnp.int32, (block, LANES), 1)
    for at in blocks:
        local = ids[at, 0, :] - offset
        positions = lax.broadcasted_iota(jnp.int32, (block, history), 1)
        local = jnp.where(positions < column(lengths[:, at]), local, -1)
        total = jnp.zeros((block, rows), jnp.float32)
        for h in range(history):
            total += jnp.where(local[:, h:h + 1] == lane_rows, 1.0, 0.0)
        counts[at, :] = total

    for i in range(len(tbl_bits)):
        pl.semaphore_wait(ready.at[i], 1)
        if i + 1 < len(tbl_bits):
            tell(i + 1)

    pltpu.make_async_copy(scales_in, scales_in, scales_recv).wait()
    for at in blocks:
        wanted = column(items[:, at])
        total = jnp.where(wanted - offset == lane_rows, row_scale, 0.0)
        for k in range(grp_n - 1):
            theirs = lax.rem(grp_i + grp_n - 1 - k, grp_n) * rows
            total += jnp.where(wanted - theirs == lane_rows, scales_in[k], 0.0)
        factors[at, :] = jnp.sum(total, axis=1, keepdims=True)

    slot = grp_i * tbl_n + tbl_i

    def give(target):
        @pl.when(target != me)
        def _():
            pltpu.make_async_remote_copy(
                src_ref=outbox.at[target], dst_ref=inbox.at[slot],
                send_sem=send_sem, recv_sem=recv_sem,
                device_id=target, device_id_type=LOGICAL,
            ).start()

    per_half = len(blocks) // 2
    for b, at in enumerate(blocks):
        half, inner = divmod(b, per_half)
        if inner == 0:
            landed = query_in.at[half]
            pltpu.make_async_copy(landed, landed, query_recv.at[half]).wait()
        asked = query[at, :]
        for k in range(grp_n - 1):
            asked += query_in[half, k, pl.ds(inner * block, block), :]
        factor = factors[at, :]
        raw = lax.dot_general(
            asked, codes[...], (((1,), (1,)), ((), ())),
            preferred_element_type=jnp.float32,
        )
        number = counts[at, :]
        score = jnp.where(number > 0.0, raw * factor * row_scale / emb, -1e30)
        peak = jnp.max(score, axis=1, keepdims=True)
        weight = number * jnp.exp(score - peak)
        mass = jnp.sum(weight, axis=1, keepdims=True)
        weight = weight * row_scale
        high = weight.astype(jnp.bfloat16)
        low = (weight - high.astype(jnp.float32)).astype(jnp.bfloat16)
        both = jnp.dot(
            jnp.concatenate([high, low], axis=0), codes[...],
            preferred_element_type=jnp.float32,
        )
        sums = both[:block] + both[block:]
        ends = jnp.where(lane == 0, peak, mass)
        for r in range(block):
            device, place = divmod(b * block + r, owned)
            outbox[device, place:place + 1, :emb] = sums[r:r + 1, :]
            outbox[device, place:place + 1, emb:] = ends[r:r + 1, :]

        if inner == per_half - 1:
            for k in range(n_dev // 2) if n_dev <= UNROLL else ():
                give(half * (n_dev // 2) + k)
            if n_dev > UNROLL:
                first = half * (n_dev // 2)
                lax.fori_loop(first, first + n_dev // 2, lambda t, c: (give(t), c)[1], 0)

    own = pltpu.make_async_copy(outbox.at[me], inbox.at[slot], recv_sem)
    own.start()
    table_load.wait()
    pltpu.make_async_copy(query_in, query_in, query_send).wait()
    pltpu.make_async_copy(scales_in, scales_in, scales_send).wait()
    pltpu.make_async_copy(inbox, inbox, recv_sem).wait()

    out_rows = lax.broadcasted_iota(jnp.int32, (tbl_n, emb), 0)
    for o in range(owned):
        shares = [inbox[pl.ds(g * tbl_n, tbl_n), o, :] for g in range(grp_n)]
        peak = shares[0][:, emb:emb + 1]
        for share in shares[1:]:
            peak = jnp.maximum(peak, share[:, emb:emb + 1])
        mass = jnp.zeros((tbl_n, 1), jnp.float32)
        sums = jnp.zeros((tbl_n, emb), jnp.float32)
        for share in shares:
            scale = jnp.exp(share[:, emb:emb + 1] - peak)
            mass += share[:, emb + 1:emb + 2] * scale
            sums += share[:, :emb] * scale
        pooled = sums / mass
        result = jnp.zeros((tbl_n, emb), jnp.float32)
        for s in range(tbl_n):
            result = jnp.where(out_rows == tables[s], pooled[s:s + 1, :], result)
        out_ref[o] = result.astype(jnp.bfloat16)
    sent = outbox.at[pl.ds(0, n_dev - 1)]
    pltpu.make_async_copy(sent, sent, send_sem).wait()


def store(pooled, out_hbm, sem):
    out = pltpu.make_async_copy(pooled, out_hbm, sem)
    out.start()
    out.wait()


def per_device(tbl_n, grp_n, codes, row_scales, history_lengths, history_ids, query_items, slot_tables):
    _, rows, emb = codes.shape
    batch, _, history = history_ids.shape
    n_dev = tbl_n * grp_n
    owned = batch // n_dev
    block = min(32, batch // 2)
    wide = emb + LANES
    hbm = pl.BlockSpec(memory_space=pl.ANY)
    pooled = pl.pallas_call(
        functools.partial(kernel, tbl_n, grp_n, block),
        out_shape=pltpu.VMEM((owned, tbl_n, emb), jnp.bfloat16),
        in_specs=[hbm] * 6,
        out_specs=pl.BlockSpec(memory_space=pltpu.VMEM),
        scratch_shapes=[
            pltpu.VMEM((rows, emb), codes.dtype),
            pltpu.VMEM((1, rows), jnp.float32),
            pltpu.VMEM((1, batch), jnp.int32),
            pltpu.VMEM((batch, 1, history), jnp.int32),
            pltpu.VMEM((1, batch), jnp.int32),
            pltpu.SMEM((tbl_n,), jnp.int32),
            pltpu.VMEM((batch, emb), jnp.bfloat16),
            pltpu.VMEM((2, grp_n - 1, batch // 2, emb), jnp.bfloat16),
            pltpu.VMEM((grp_n - 1, 1, rows), jnp.float32),
            pltpu.VMEM((batch, 1), jnp.float32),
            pltpu.VMEM((batch, rows), jnp.float32),
            pltpu.VMEM((n_dev, owned, wide), jnp.float32),
            pltpu.VMEM((n_dev, owned, wide), jnp.float32),
            pltpu.SemaphoreType.DMA((5,)),
            pltpu.SemaphoreType.DMA,
            pltpu.SemaphoreType.DMA,
            pltpu.SemaphoreType.DMA((2,)),
            pltpu.SemaphoreType.DMA,
            pltpu.SemaphoreType.DMA,
            pltpu.SemaphoreType.DMA,
            pltpu.SemaphoreType.DMA,
            pltpu.SemaphoreType.REGULAR((tbl_n.bit_length() - 1,)),
        ],
        compiler_params=pltpu.CompilerParams(collective_id=0, has_side_effects=True),
    )(
        codes.reshape(rows, emb), row_scales, history_lengths.T, history_ids,
        query_items.T, slot_tables,
    )
    return pl.pallas_call(
        store,
        out_shape=jax.ShapeDtypeStruct((owned, tbl_n, emb), jnp.bfloat16),
        in_specs=[pl.BlockSpec(memory_space=pltpu.VMEM)],
        out_specs=pl.BlockSpec(memory_space=pl.ANY),
        scratch_shapes=[pltpu.SemaphoreType.DMA],
    )(pltpu.with_memory_space_constraint(pooled, pltpu.VMEM))


def solution(mesh):
    placed = (
        P("tbl", "grp", None),
        P("tbl", "grp"),
        P(None, "tbl"),
        P(None, "tbl", None),
        P(None, "tbl"),
        P(),
    )
    return jax.shard_map(
        functools.partial(per_device, mesh.shape["tbl"], mesh.shape["grp"]),
        mesh=mesh,
        in_specs=placed,
        out_specs=P(("tbl", "grp"), None, None),
        check_vma=False,
    )
```
